32 devices in a mesh: shot: 2 (over y), tile: 4 (over z), slab: 4 (over x, core).
Axes of the slice: x: 2, y: 2, z: 4, core: 2. Of those that a mesh axis runs over, the one named last changes fastest.
Arguments:
- source_field: float32 [8, 2, 64, 256], P('shot', None, 'tile'), parts along dimension 0, may hold values from -6 to 6
- receiver_field: float32 [8, 2, 64, 256], P('shot', None, 'tile'), parts along dimension 0, may hold values from -6 to 6
- velocity_index: int32 [8, 64, 256], P(('shot', 'slab'), 'tile'), parts along dimension 0, may hold values from 0 to 31
- coefficient_table: float32 [4, 2, 10, 32], replicated, may hold values from -1.5 to 1.5
Outputs:
- imaged: float32 [8, 64, 256], P(('shot', 'slab'), 'tile'), parts along dimension 0
The draws below stay inside these ranges and needn't reach their ends.
There are 2 independent parts, one for each index of `shot`. The reference program is written for one: setup_inputs(seed, part) draws one part's arguments, and reference() takes and returns one part's arrays. A program takes and returns all parts, laid end to end along the dimension named above; an argument that names none is the same for every part. Nothing has to cross between parts.
All inputs are finite; a program needn't handle non-finite values.
Results may differ from the reference program's by a relative error of at most 0.0003.
Values sent between devices are 32-bit elements; how exact they have to be, the bound alone decides.
A program may use at most 64 MiB of HBM per device.

```python
import jax
import jax.numpy as jnp

NY = 256
FREQS = 4
TERMS = 10
BINS = 32
NX = 64
DEPTH = 4


def set_ends(entries, own_key, least, high):
    index_at = [jax.random.randint(jax.random.fold_in(own_key, axis), (), 0, length) for axis, length in enumerate(entries.shape)]
    longest = entries.shape.index(max(entries.shape))
    next_to = index_at[:longest] + [(index_at[longest] + 1) % entries.shape[longest]] + index_at[longest + 1:]
    return entries.at[tuple(index_at)].set(least).at[tuple(next_to)].set(high)


def steps_of(rng, shape, pieces, low, largest):
    gain = 1.0
    for axis_at, blocks in pieces:
        steps = jax.random.uniform(jax.random.fold_in(jax.random.fold_in(rng, 6), axis_at), (blocks,), jnp.float32, low / len(pieces), largest / len(pieces))
        gain = gain * jnp.repeat(jnp.exp(steps), shape[axis_at] // blocks).reshape((-1,) + (1,) * (len(shape) - 1 - axis_at))
    return gain


def scatter_about(key, shape, deviation, reach, pieces=(), kind=jnp.bfloat16):
    entries = deviation * jax.random.normal(key, shape, jnp.float32)
    if pieces:
        entries = entries * steps_of(key, shape, pieces, -0.22, 0.18)
    return jnp.clip(entries, -reach, reach).astype(kind)


def setup_inputs(seed: int = 0, part: int = 0) -> dict:
    splits = jax.random.split(jax.random.key(seed), 5)
    part_keys = jax.random.split(jax.random.fold_in(splits[4], part), 5)
    source_field = scatter_about(part_keys[0], (FREQS, 2, NX, NY), 1.0, 6.0, ((2, 4),), jnp.float32)
    receiver_field = scatter_about(part_keys[1], (FREQS, 2, NX, NY), 1.0, 6.0, ((2, 4),), jnp.float32)
    velocity_index = set_ends(jax.random.randint(part_keys[2], (DEPTH, NX, NY), 0, BINS), jax.random.fold_in(part_keys[2], 1), 0, BINS - 1).astype(jnp.int32)
    coefficient_table = scatter_about(splits[3], (FREQS, 2, TERMS, BINS), 0.3, 1.5, (), jnp.float32)
    return dict(source_field=source_field, receiver_field=receiver_field, velocity_index=velocity_index, coefficient_table=coefficient_table)


def mcclellan(field):
    dim_count = field.ndim
    padded = jnp.pad(field, [(0, 0)] * (dim_count - 2) + [(1, 1), (0, 0)])
    across = 0.5 * field + 0.25 * (padded[..., :-2, :] + padded[..., 2:, :])
    sideways = jnp.pad(across, [(0, 0)] * (dim_count - 1) + [(1, 1)])
    combined = 0.5 * across + 0.25 * (sideways[..., :-2] + sideways[..., 2:])
    return 2.0 * combined - field


def accumulate(summed, term_field, coeffs):
    field_sign = jnp.array([-1.0, 1.0], dtype=jnp.float32).reshape(2, 1, 1)
    real_part = coeffs[:, 0][:, None]
    imag_part = coeffs[:, 1][:, None] * field_sign
    real_out = real_part * term_field[:, :, 0] - imag_part * term_field[:, :, 1]
    imag_out = real_part * term_field[:, :, 1] + imag_part * term_field[:, :, 0]
    return summed + jnp.stack([real_out, imag_out], axis=2)


def extrapolate(fields, coeffs):
    earlier = fields
    current_term = mcclellan(fields)
    summed = accumulate(jnp.zeros_like(fields), earlier, coeffs[:, :, 0])
    summed = accumulate(summed, current_term, coeffs[:, :, 1])
    for term_index in range(2, TERMS):
        following = 2.0 * mcclellan(current_term) - earlier
        summed = accumulate(summed, following, coeffs[:, :, term_index])
        earlier, current_term = current_term, following
    return summed


def correlate(fields):
    return jnp.sum(fields[:, 0, 0] * fields[:, 1, 0] + fields[:, 0, 1] * fields[:, 1, 1], axis=0)


def reference(source_field, receiver_field, velocity_index, coefficient_table):
    fields = jnp.stack([source_field, receiver_field], axis=1)
    images = []
    for depth_step in range(DEPTH):
        coeffs = jnp.take(coefficient_table, velocity_index[depth_step], axis=3)
        fields = extrapolate(fields, coeffs)
        images.append(correlate(fields))
    return jnp.stack(images, axis=0)
```

```python
import functools

import jax
import jax.numpy as jnp
from jax import lax
from jax.experimental import pallas as pl
from jax.experimental.pallas import tpu as pltpu
from jax.sharding import PartitionSpec as P

MESH = pl.DeviceIdType.MESH


def lane_gather(values, index):
    dims = lax.GatherDimensionNumbers(
        offset_dims=(),
        collapsed_slice_dims=(1,),
        start_index_map=(1,),
        operand_batching_dims=(0,),
        start_indices_batching_dims=(0,),
    )
    return lax.gather(
        values, index[..., None], dims, (1, 1), mode=lax.GatherScatterMode.PROMISE_IN_BOUNDS
    )


def stencil(x):
    shape = x[0].shape
    sub = lax.broadcasted_iota(jnp.int32, shape, 1)
    lane = lax.broadcasted_iota(jnp.int32, shape, 2)
    zero = jnp.zeros((1,) + shape[1:], jnp.float32)
    rows = []
    for v in x:
        rot = pltpu.roll(v, 1, 1)
        before = jnp.concatenate([zero, rot[:-1]], axis=0)
        u = v + jnp.where(sub == 0, before, rot)
        rot = pltpu.roll(u, 7, 1)
        after = jnp.concatenate([rot[1:], v[-1:]], axis=0)
        rows.append(u + jnp.where(sub == 7, after, rot))
    low, high = rows
    rot_low, rot_high = pltpu.roll(low, 1, 2), pltpu.roll(high, 1, 2)
    u_low = low + jnp.where(lane == 0, 0.0, rot_low)
    u_high = high + jnp.where(lane == 0, rot_low, rot_high)
    rot_low, rot_high = pltpu.roll(u_low, 127, 2), pltpu.roll(u_high, 127, 2)
    return [
        u_low + jnp.where(lane == 127, rot_high, rot_low),
        u_high + jnp.where(lane == 127, high, rot_high),
    ]


def kernel(
    n, slabs, w, trows, terms,
    src_ref, rcv_ref, v_ref, tab_ref, out_ref,
    fld, tst, vel, tabs, other, part, contrib,
    loc_sem, fs_sem, fr_sem, v1s_sem, v1r_sem, v2s_sem, v2r_sem, xs_sem, xr_sem, cs_sem, cr_sem,
):
    wr = w * trows
    nb = wr // 8
    t, s = lax.axis_index("tile"), lax.axis_index("slab")
    role, low = lax.rem(s, 2), lax.rem(t, 2)
    pair = t - low
    group = s - role
    freq = group + low

    def base(tile):
        first = tile - lax.rem(tile, 2)
        return jnp.clip(first - 3, 0, n - w)

    own = t - base(t)

    def rows(slot):
        return pl.ds(pl.multiple_of(slot * trows, 8), trows)

    if w == n:
        others = [(lax.rem(t + j, n), None, None) for j in range(1, n)]
    else:
        others = []
        for delta in range(-(w - 1), w):
            if delta:
                u = t + delta
                there = (u >= 0) & (u < n)
                safe = jnp.clip(u, 0, n - 1)
                slot = t - base(safe)
                others.append((safe, there, there & (slot >= 0) & (slot < w)))

    def when(cond, body):
        if cond is None:
            body()
        else:
            pl.when(cond)(body)

    barrier = pltpu.get_barrier_semaphore()
    count = 0
    for u, there, _ in others:
        def hello(u=u):
            pl.semaphore_signal(barrier, inc=1, device_id={"tile": u}, device_id_type=MESH)
        when(there, hello)
    for b in range(2):
        for j in range(1, slabs):
            pl.semaphore_signal(
                barrier, inc=1, device_id={"tile": pair + b, "slab": lax.rem(s + j, slabs)}, device_id_type=MESH
            )
    if w == n:
        count = n - 1
    else:
        count = jnp.minimum(t, w - 1) + jnp.minimum(n - 1 - t, w - 1)

    loc_v = pltpu.make_async_copy(v_ref.at[0], vel.at[s, rows(own)], loc_sem.at[0])
    loc_v.start()
    def own_field(ref):
        return pltpu.make_async_copy(ref.at[freq], fld.at[0, :, rows(own)], loc_sem.at[1])
    pl.when(role == 0)(lambda: own_field(src_ref).start())
    pl.when(role == 1)(lambda: own_field(rcv_ref).start())

    pl.semaphore_wait(barrier, count + 2 * (slabs - 1))

    v1 = []
    for j in range(1, slabs):
        copy = pltpu.make_async_remote_copy(
            v_ref.at[0], vel.at[s, rows(own)], v1s_sem.at[j], v1r_sem.at[s],
            device_id={"slab": lax.rem(s + j, slabs)}, device_id_type=MESH,
        )
        copy.start()
        v1.append(copy)

    def field_copy(ref, j, u):
        return pltpu.make_async_remote_copy(
            ref.at[group + lax.rem(u, 2)], fld.at[0, :, rows(t - base(u))],
            fs_sem.at[j], fr_sem.at[t - base(u)], device_id={"tile": u}, device_id_type=MESH,
        )

    for j, (u, _, needs) in enumerate(others):
        def send(j=j, u=u):
            pl.when(role == 0)(lambda: field_copy(src_ref, j, u).start())
            pl.when(role == 1)(lambda: field_copy(rcv_ref, j, u).start())
        when(needs, send)

    loc_v.wait()

    def vel_copy(d, j, u):
        return pltpu.make_async_remote_copy(
            vel.at[d, rows(own)], vel.at[d, rows(t - base(u))],
            v2s_sem.at[d, j], v2r_sem.at[d, t - base(u)], device_id={"tile": u}, device_id_type=MESH,
        )

    for d in range(slabs):
        @pl.when(s != d)
        def _():
            pltpu.make_async_remote_copy(
                v_ref.at[0], vel.at[d, rows(own)], v1s_sem.at[0], v1r_sem.at[d],
                device_id={"slab": lax.rem(s + 1, slabs)}, device_id_type=MESH,
            ).wait_recv()
        for j, (u, _, needs) in enumerate(others):
            when(needs, lambda d=d, j=j, u=u: vel_copy(d, j, u).start())

    sign = jnp.where(role == 0, -1.0, 1.0).astype(jnp.float32)
    bins = tab_ref.shape[3]
    tabs[...] = jnp.zeros_like(tabs)
    for p in range(2):
        for k in range(terms):
            row = tab_ref[freq, p, pl.ds(k, 1), :]
            if p:
                row = row * sign
            tabs[p * terms + k, :, pl.ds(0, bins)] = jnp.broadcast_to(row, (8, bins))

    own_field(src_ref).wait()
    for j in range(1, w):
        slot = lax.rem(own + j, w)
        pltpu.make_async_remote_copy(
            src_ref.at[0], fld.at[0, :, rows(slot)], fs_sem.at[0], fr_sem.at[slot],
            device_id={"tile": others[0][0]}, device_id_type=MESH,
        ).wait_recv()

    def advance(d):
        def series(c, _):
            halves = [
                fld[d, c, :, pl.ds(128 * h, 128)].reshape(nb, 8, 128) for h in range(2)
            ]
            term, change = halves, None
            for k in range(1, terms):
                spread = stencil(term)
                if k == 1:
                    change = [0.125 * b for b in spread]
                else:
                    change = [0.25 * b - e for b, e in zip(spread, change)]
                term = [e - x for e, x in zip(change, term)]
                for h in range(2):
                    tst[k - 1, c, :, pl.ds(128 * h, 128)] = term[h].reshape(wr, 128)
            return 0

        lax.fori_loop(0, 2, series, 0)
        for j in range(1, w):
            slot = lax.rem(own + j, w)
            pltpu.make_async_remote_copy(
                vel.at[d, rows(own)], vel.at[d, rows(slot)], v2s_sem.at[d, 0], v2r_sem.at[d, slot],
                device_id={"tile": others[0][0]}, device_id_type=MESH,
            ).wait_recv()

        def gather(i, _):
            block = pl.ds(pl.multiple_of(i * 8, 8), 8)
            for h in range(2):
                lanes = pl.ds(128 * h, 128)
                index = vel[d, block, lanes]
                real = imag = None
                for k in range(terms):
                    c_real = lane_gather(tabs[k], index)
                    c_imag = lane_gather(tabs[terms + k], index)
                    t_real = fld[d, 0, block, lanes] if k == 0 else tst[k - 1, 0, block, lanes]
                    t_imag = fld[d, 1, block, lanes] if k == 0 else tst[k - 1, 1, block, lanes]
                    add_real = c_real * t_real - c_imag * t_imag
                    add_imag = c_real * t_imag + c_imag * t_real
                    real = add_real if real is None else real + add_real
                    imag = add_imag if imag is None else imag + add_imag
                fld[d + 1, 0, block, lanes] = real
                fld[d + 1, 1, block, lanes] = imag
            return 0

        lax.fori_loop(0, nb, gather, 0)

    mine = rows(pair + role - base(t))
    theirs = rows(pair + (1 - role) - base(t))
    partner = group + (1 - role)
    place = lax.div(s, 2) * 2 + low

    def swap(d):
        return pltpu.make_async_remote_copy(
            fld.at[d + 1, :, theirs], other.at[d], xs_sem.at[d], xr_sem.at[d],
            device_id={"slab": partner}, device_id_type=MESH,
        )

    def deliver(d):
        return pltpu.make_async_remote_copy(
            part.at[d], contrib.at[place], cs_sem.at[d], cr_sem.at[place],
            device_id={"tile": pair + role, "slab": d}, device_id_type=MESH,
        )

    stays = low == role

    def image(d):
        swap(d).wait_recv()
        product = fld[d + 1, 0, mine, :] * other[d, 0] + fld[d + 1, 1, mine, :] * other[d, 1]
        home = stays & (s == d)
        @pl.when(home)
        def _():
            contrib[place] = product
        @pl.when(jnp.logical_not(home))
        def _():
            part[d] = product
            deliver(d).start()

    for d in range(slabs):
        advance(d)
        swap(d).start()
        if d:
            image(d - 1)
    image(slabs - 1)

    for q in range(slabs):
        local = (place == q) & stays
        @pl.when(jnp.logical_not(local))
        def _():
            pltpu.make_async_remote_copy(
                part.at[0], contrib.at[q], cs_sem.at[0], cr_sem.at[q],
                device_id={"slab": partner}, device_id_type=MESH,
            ).wait_recv()
    total = contrib[0]
    for q in range(1, slabs):
        total = total + contrib[q]
    out_ref[0] = total

    for copy in v1:
        copy.wait_send()
    for j, (u, _, needs) in enumerate(others):
        def left(j=j, u=u):
            field_copy(src_ref, j, u).wait_send()
            for d in range(slabs):
                vel_copy(d, j, u).wait_send()
        when(needs, left)
    for d in range(slabs):
        swap(d).wait_send()
        pl.when(jnp.logical_not(stays & (s == d)))(lambda d=d: deliver(d).wait_send())


def solution(mesh):
    n, slabs = mesh.shape["tile"], mesh.shape["slab"]

    def local(source_field, receiver_field, velocity_index, coefficient_table):
        terms = coefficient_table.shape[2]
        trows, ny = velocity_index.shape[1:]
        reach = -(-(slabs * (terms - 1)) // trows)
        w = min(n, 2 * reach + 2)
        assert source_field.shape[0] == slabs == 4 and n % 2 == 0 and ny == 256
        assert reach == 3 and trows % 8 == 0
        wr = w * trows
        peers = n - 1 if w == n else 2 * (w - 1)
        dma = pltpu.SemaphoreType.DMA
        anywhere = pl.BlockSpec(memory_space=pl.ANY)
        vmem = pl.BlockSpec(memory_space=pltpu.VMEM)
        return pl.pallas_call(
            functools.partial(kernel, n, slabs, w, trows, terms),
            out_shape=jax.ShapeDtypeStruct((1, trows, ny), jnp.float32),
            in_specs=[anywhere, anywhere, anywhere, vmem],
            out_specs=vmem,
            scratch_shapes=[
                pltpu.VMEM((slabs + 1, 2, wr, ny), jnp.float32),
                pltpu.VMEM((terms - 1, 2, wr, ny), jnp.float32),
                pltpu.VMEM((slabs, wr, ny), jnp.int32),
                pltpu.VMEM((2 * terms, 8, 128), jnp.float32),
                pltpu.VMEM((slabs, 2, trows, ny), jnp.float32),
                pltpu.VMEM((slabs, trows, ny), jnp.float32),
                pltpu.VMEM((slabs, trows, ny), jnp.float32),
                dma((2,)),
                dma((peers,)),
                dma((w,)),
                dma((slabs,)),
                dma((slabs,)),
                dma((slabs, peers)),
                dma((slabs, w)),
                dma((slabs,)),
                dma((slabs,)),
                dma((slabs,)),
                dma((slabs,)),
            ],
            compiler_params=pltpu.CompilerParams(collective_id=0, has_side_effects=True),
            name="migrate",
        )(source_field, receiver_field, velocity_index, coefficient_table)

    return jax.shard_map(
        local,
        mesh=mesh,
        in_specs=(
            P("shot", None, "tile", None),
            P("shot", None, "tile", None),
            P(("shot", "slab"), "tile", None),
            P(),
        ),
        out_specs=P(("shot", "slab"), "tile", None),
        check_vma=False,
    )
```

```python
import functools

import jax
import jax.numpy as jnp
from jax import lax
from jax.experimental import pallas as pl
from jax.experimental.pallas import tpu as pltpu
from jax.sharding import PartitionSpec as P

MESH = pl.DeviceIdType.MESH
GROUP = 4


def lane_gather(values, index):
    dims = lax.GatherDimensionNumbers(
        offset_dims=(),
        collapsed_slice_dims=(1,),
        start_index_map=(1,),
        operand_batching_dims=(0,),
        start_indices_batching_dims=(0,),
    )
    return lax.gather(
        values, index[..., None], dims, (1, 1), mode=lax.GatherScatterMode.PROMISE_IN_BOUNDS
    )


def split_lanes(low, high):
    lane = lax.broadcasted_iota(jnp.int32, (8, 128), 1)
    even = lax.rem(2 * lane, 128)
    return [
        jnp.where(lane < 64, lane_gather(low, even + p), lane_gather(high, even + p)) for p in range(2)
    ]


def merge_lanes(even, odd):
    lane = lax.broadcasted_iota(jnp.int32, (8, 128), 1)
    half = lax.div(lane, 2)
    first = lax.rem(lane, 2) == 0
    return [
        jnp.where(first, lane_gather(even, half + q), lane_gather(odd, half + q)) for q in (0, 64)
    ]


def stencil(x):
    sub = lax.broadcasted_iota(jnp.int32, (8, 128), 0)
    lane = lax.broadcasted_iota(jnp.int32, x[0].shape, 2)
    rows = []
    for v in x:
        top = jnp.where(sub == 0, 0.0, pltpu.roll(v[-1], 1, 0))
        u = v + jnp.concatenate([top[None], v[:-1]], axis=0)
        end = jnp.where(sub == 7, v[-1], pltpu.roll(u[0], 7, 0))
        rows.append(u + jnp.concatenate([u[1:], end[None]], axis=0))
    even, odd = rows
    u_odd = odd + even
    u_even = even + jnp.where(lane == 0, 0.0, pltpu.roll(odd, 1, 2))
    return [u_even + u_odd, u_odd + jnp.where(lane == 127, odd, pltpu.roll(u_even, 127, 2))]


def kernel(
    n, slabs, w, trows, terms,
    src_ref, rcv_ref, v_ref, tab_ref, out_ref,
    surf, fld, tst, vel, bins_at, tabs, other, part, contrib,
    loc_sem, fs_sem, fr_sem, v1s_sem, v1r_sem, v2s_sem, v2r_sem, xs_sem, xr_sem, cs_sem, cr_sem,
):
    wr = w * trows
    nb = wr // 8
    t, s = lax.axis_index("tile"), lax.axis_index("slab")
    role, low = lax.rem(s, 2), lax.rem(t, 2)
    pair = t - low
    group = s - role
    partner = group + (1 - role)
    freq = group + low

    def base(tile):
        first = tile - lax.rem(tile, 2)
        return jnp.clip(first - 3, 0, n - w)

    own = t - base(t)

    def rows(slot):
        return pl.ds(pl.multiple_of(slot * trows, 8), trows)

    if w == n:
        others = [(lax.rem(t + j, n), None, None) for j in range(1, n)]
    else:
        others = []
        for delta in range(-(w - 1), w):
            if delta:
                u = t + delta
                there = (u >= 0) & (u < n)
                safe = jnp.clip(u, 0, n - 1)
                slot = t - base(safe)
                others.append((safe, there, there & (slot >= 0) & (slot < w)))

    def when(cond, body):
        if cond is None:
            body()
        else:
            pl.when(cond)(body)

    barrier = pltpu.get_barrier_semaphore()
    count = 0
    for u, there, _ in others:
        def hello(u=u):
            pl.semaphore_signal(barrier, inc=1, device_id={"tile": u}, device_id_type=MESH)
        when(there, hello)
    for b in range(2):
        for j in range(1, slabs):
            pl.semaphore_signal(
                barrier, inc=1, device_id={"tile": pair + b, "slab": lax.rem(s + j, slabs)}, device_id_type=MESH
            )
    if w == n:
        count = n - 1
    else:
        count = jnp.minimum(t, w - 1) + jnp.minimum(n - 1 - t, w - 1)

    loc_v = pltpu.make_async_copy(v_ref.at[0], vel.at[s, rows(own)], loc_sem.at[0])
    loc_v.start()
    def own_field(ref):
        return pltpu.make_async_copy(ref.at[freq], surf.at[:, rows(own)], loc_sem.at[1])
    pl.when(role == 0)(lambda: own_field(src_ref).start())
    pl.when(role == 1)(lambda: own_field(rcv_ref).start())

    sign = jnp.where(role == 0, -1.0, 1.0).astype(jnp.float32)
    bins = tab_ref.shape[3]
    tabs[...] = jnp.zeros_like(tabs)
    for p in range(2):
        for k in range(terms):
            row = tab_ref[freq, k, pl.ds(p, 1), :]
            if p:
                row = row * sign
            tabs[p * terms + k, :, pl.ds(0, bins)] = jnp.broadcast_to(row, (8, bins))

    pl.semaphore_wait(barrier, count + 2 * (slabs - 1))

    def vel_copy(j, u):
        return pltpu.make_async_remote_copy(
            v_ref.at[0], vel.at[s, rows(t - base(u))], v1s_sem.at[j], v1r_sem.at[t - base(u)],
            device_id={"tile": u}, device_id_type=MESH,
        )

    for j, (u, _, needs) in enumerate(others):
        when(needs, lambda j=j, u=u: vel_copy(j, u).start())

    def field_copy(ref, j, u):
        return pltpu.make_async_remote_copy(
            ref.at[group + lax.rem(u, 2)], surf.at[:, rows(t - base(u))],
            fs_sem.at[j], fr_sem.at[t - base(u)], device_id={"tile": u}, device_id_type=MESH,
        )

    for j, (u, _, needs) in enumerate(others):
        def send(j=j, u=u):
            pl.when(role == 0)(lambda: field_copy(src_ref, j, u).start())
            pl.when(role == 1)(lambda: field_copy(rcv_ref, j, u).start())
        when(needs, send)

    loc_v.wait()
    for j in range(1, w):
        slot = lax.rem(own + j, w)
        pltpu.make_async_remote_copy(
            v_ref.at[0], vel.at[s, rows(slot)], v1s_sem.at[0], v1r_sem.at[slot],
            device_id={"tile": others[0][0]}, device_id_type=MESH,
        ).wait_recv()
    v2 = []
    for j in range(1, slabs):
        copy = pltpu.make_async_remote_copy(
            vel.at[s], vel.at[s], v2s_sem.at[j], v2r_sem.at[s],
            device_id={"slab": lax.rem(s + j, slabs)}, device_id_type=MESH,
        )
        copy.start()
        v2.append(copy)

    own_field(src_ref).wait()
    for j in range(1, w):
        slot = lax.rem(own + j, w)
        pltpu.make_async_remote_copy(
            src_ref.at[0], surf.at[:, rows(slot)], fs_sem.at[0], fr_sem.at[slot],
            device_id={"tile": others[0][0]}, device_id_type=MESH,
        ).wait_recv()

    def advance(d):
        if d == 0:
            for c in range(2):
                for b in range(nb):
                    block = pl.ds(8 * b, 8)
                    even, odd = split_lanes(surf[c, block, pl.ds(0, 128)], surf[c, block, pl.ds(128, 128)])
                    fld[0, c, 0, block, :] = even
                    fld[0, c, 1, block, :] = odd
        terms_of = [
            [
                jnp.concatenate([fld[d, c, h, pl.ds(b, 8, stride=nb), :][None] for b in range(nb)], axis=0)
                for h in range(2)
            ]
            for c in range(2)
        ]
        changes = [None, None]
        for k in range(terms):
            for c in range(2):
                if k:
                    spread = stencil(terms_of[c])
                    if k == 1:
                        changes[c] = [0.125 * b for b in spread]
                    else:
                        changes[c] = [0.25 * b - e for b, e in zip(spread, changes[c])]
                    terms_of[c] = [e - x for e, x in zip(changes[c], terms_of[c])]
                for h in range(2):
                    tst[k, c, :, :, pl.ds(128 * h, 128)] = terms_of[c][h]

        @pl.when(s != d)
        def _():
            pltpu.make_async_remote_copy(
                vel.at[d], vel.at[d], v2s_sem.at[0], v2r_sem.at[d],
                device_id={"slab": partner}, device_id_type=MESH,
            ).wait_recv()

        for b in range(nb):
            block = pl.ds(8 * b, 8)
            even, odd = split_lanes(vel[d, block, pl.ds(0, 128)], vel[d, block, pl.ds(128, 128)])
            bins_at[0, block, :] = even
            bins_at[1, block, :] = odd

        def gather(i, _):
            for bb in range(GROUP):
                b = i * GROUP + bb
                block = pl.ds(b, 8, stride=nb)
                for h in range(2):
                    lanes = pl.ds(128 * h, 128)
                    index = bins_at[h, block, :]
                    real = imag = None
                    for k in range(terms):
                        c_real = lane_gather(tabs[k], index)
                        c_imag = lane_gather(tabs[terms + k], index)
                        t_real = tst[k, 0, b, :, lanes]
                        t_imag = tst[k, 1, b, :, lanes]
                        add_real = c_real * t_real - c_imag * t_imag
                        add_imag = c_real * t_imag + c_imag * t_real
                        real = add_real if real is None else real + add_real
                        imag = add_imag if imag is None else imag + add_imag
                    fld[d + 1, 0, h, block, :] = real
                    fld[d + 1, 1, h, block, :] = imag
            return 0

        lax.fori_loop(0, nb // GROUP, gather, 0)

    mine = rows(pair + role - base(t))
    theirs = rows(pair + (1 - role) - base(t))
    place = lax.div(s, 2) * 2 + low

    def swap(d):
        return pltpu.make_async_remote_copy(
            fld.at[d + 1, :, :, theirs], other.at[d], xs_sem.at[d], xr_sem.at[d],
            device_id={"slab": partner}, device_id_type=MESH,
        )

    def deliver(d):
        return pltpu.make_async_remote_copy(
            part.at[d], contrib.at[place], cs_sem.at[d], cr_sem.at[place],
            device_id={"tile": pair + role, "slab": d}, device_id_type=MESH,
        )

    stays = low == role

    def image(d):
        swap(d).wait_recv()
        product = fld[d + 1, 0, :, mine, :] * other[d, 0] + fld[d + 1, 1, :, mine, :] * other[d, 1]
        home = stays & (s == d)
        @pl.when(home)
        def _():
            contrib[place] = product
        @pl.when(jnp.logical_not(home))
        def _():
            part[d] = product
            deliver(d).start()

    for d in range(slabs):
        advance(d)
        swap(d).start()
        if d:
            image(d - 1)
    image(slabs - 1)

    for q in range(slabs):
        local = (place == q) & stays
        @pl.when(jnp.logical_not(local))
        def _():
            pltpu.make_async_remote_copy(
                part.at[0], contrib.at[q], cs_sem.at[0], cr_sem.at[q],
                device_id={"slab": partner}, device_id_type=MESH,
            ).wait_recv()
    total = contrib[0]
    for q in range(1, slabs):
        total = total + contrib[q]
    for b in range(trows // 8):
        block = pl.ds(8 * b, 8)
        low_half, high_half = merge_lanes(total[0, 8 * b : 8 * b + 8], total[1, 8 * b : 8 * b + 8])
        out_ref[0, block, pl.ds(0, 128)] = low_half
        out_ref[0, block, pl.ds(128, 128)] = high_half

    for copy in v2:
        copy.wait_send()
    for j, (u, _, needs) in enumerate(others):
        def left(j=j, u=u):
            field_copy(src_ref, j, u).wait_send()
            vel_copy(j, u).wait_send()
        when(needs, left)
    for d in range(slabs):
        swap(d).wait_send()
        pl.when(jnp.logical_not(stays & (s == d)))(lambda d=d: deliver(d).wait_send())


def solution(mesh):
    n, slabs = mesh.shape["tile"], mesh.shape["slab"]

    def local(source_field, receiver_field, velocity_index, coefficient_table):
        terms = coefficient_table.shape[2]
        trows, ny = velocity_index.shape[1:]
        reach = -(-(slabs * (terms - 1)) // trows)
        w = min(n, 2 * reach + 2)
        assert source_field.shape[0] == slabs == 4 and n % 2 == 0 and ny == 256
        assert reach == 3 and trows % 8 == 0
        wr = w * trows
        peers = n - 1 if w == n else 2 * (w - 1)
        dma = pltpu.SemaphoreType.DMA
        anywhere = pl.BlockSpec(memory_space=pl.ANY)
        vmem = pl.BlockSpec(memory_space=pltpu.VMEM)
        return pl.pallas_call(
            functools.partial(kernel, n, slabs, w, trows, terms),
            out_shape=jax.ShapeDtypeStruct((1, trows, ny), jnp.float32),
            in_specs=[anywhere, anywhere, anywhere, vmem],
            out_specs=vmem,
            scratch_shapes=[
                pltpu.VMEM((2, wr, ny), jnp.float32),
                pltpu.VMEM((slabs + 1, 2, 2, wr, ny // 2), jnp.float32),
                pltpu.VMEM((terms, 2, wr // 8, 8, ny), jnp.float32),
                pltpu.VMEM((slabs, wr, ny), jnp.int32),
                pltpu.VMEM((2, wr, ny // 2), jnp.int32),
                pltpu.VMEM((2 * terms, 8, 128), jnp.float32),
                pltpu.VMEM((slabs, 2, 2, trows, ny // 2), jnp.float32),
                pltpu.VMEM((slabs, 2, trows, ny // 2), jnp.float32),
                pltpu.VMEM((slabs, 2, trows, ny // 2), jnp.float32),
                dma((2,)),
                dma((peers,)),
                dma((w,)),
                dma((peers,)),
                dma((w,)),
                dma((slabs,)),
                dma((slabs,)),
                dma((slabs,)),
                dma((slabs,)),
                dma((slabs,)),
                dma((slabs,)),
            ],
            compiler_params=pltpu.CompilerParams(collective_id=0, has_side_effects=True),
            name="migrate",
        )(source_field, receiver_field, velocity_index, jnp.transpose(coefficient_table, (0, 2, 1, 3)))

    return jax.shard_map(
        local,
        mesh=mesh,
        in_specs=(
            P("shot", None, "tile", None),
            P("shot", None, "tile", None),
            P(("shot", "slab"), "tile", None),
            P(),
        ),
        out_specs=P(("shot", "slab"), "tile", None),
        check_vma=False,
    )
```

```python
import functools

import jax
import jax.numpy as jnp
from jax import lax
from jax.experimental import pallas as pl
from jax.experimental.pallas import tpu as pltpu
from jax.sharding import PartitionSpec as P

MESH = pl.DeviceIdType.MESH
GROUP = 4


def lane_gather(values, index):
    dims = lax.GatherDimensionNumbers(
        offset_dims=(),
        collapsed_slice_dims=(1,),
        start_index_map=(1,),
        operand_batching_dims=(0,),
        start_indices_batching_dims=(0,),
    )
    return lax.gather(
        values, index[..., None], dims, (1, 1), mode=lax.GatherScatterMode.PROMISE_IN_BOUNDS
    )


def split_lanes(low, high):
    lane = lax.broadcasted_iota(jnp.int32, (8, 128), 1)
    even = lax.rem(2 * lane, 128)
    return [
        jnp.where(lane < 64, lane_gather(low, even + p), lane_gather(high, even + p)) for p in range(2)
    ]


def merge_lanes(even, odd):
    lane = lax.broadcasted_iota(jnp.int32, (8, 128), 1)
    half = lax.div(lane, 2)
    first = lax.rem(lane, 2) == 0
    return [
        jnp.where(first, lane_gather(even, half + q), lane_gather(odd, half + q)) for q in (0, 64)
    ]


def stencil(x):
    sub = lax.broadcasted_iota(jnp.int32, (8, 128), 0)
    lane = lax.broadcasted_iota(jnp.int32, x[0].shape, 2)
    rows = []
    for v in x:
        top = jnp.where(sub == 0, 0.0, pltpu.roll(v[-1], 1, 0))
        u = v + jnp.concatenate([top[None], v[:-1]], axis=0)
        end = jnp.where(sub == 7, v[-1], pltpu.roll(u[0], 7, 0))
        rows.append(u + jnp.concatenate([u[1:], end[None]], axis=0))
    even, odd = rows
    u_odd = odd + even
    u_even = even + jnp.where(lane == 0, 0.0, pltpu.roll(odd, 1, 2))
    return [u_even + u_odd, u_odd + jnp.where(lane == 127, odd, pltpu.roll(u_even, 127, 2))]


def kernel(
    n, slabs, w, trows, terms,
    src_ref, rcv_ref, v_ref, tab_ref, out_ref,
    surf, fld, tst, vel, bins_at, tabs, other, part, contrib,
    loc_sem, fs_sem, fr_sem, v1s_sem, v1r_sem, v2s_sem, v2r_sem, xs_sem, xr_sem, cs_sem, cr_sem,
):
    wr = w * trows
    nb = wr // 8
    t, s = lax.axis_index("tile"), lax.axis_index("slab")
    role, low = lax.rem(s, 2), lax.rem(t, 2)
    pair = t - low
    group = s - role
    partner = group + (1 - role)
    freq = group + low

    def base(tile):
        first = tile - lax.rem(tile, 2)
        return jnp.clip(first - 3, 0, n - w)

    own = t - base(t)

    def rows(slot):
        return pl.ds(pl.multiple_of(slot * trows, 8), trows)

    if w == n:
        others = [(lax.rem(t + j, n), None, None) for j in range(1, n)]
    else:
        others = []
        for delta in range(-(w - 1), w):
            if delta:
                u = t + delta
                there = (u >= 0) & (u < n)
                safe = jnp.clip(u, 0, n - 1)
                slot = t - base(safe)
                others.append((safe, there, there & (slot >= 0) & (slot < w)))

    def when(cond, body):
        if cond is None:
            body()
        else:
            pl.when(cond)(body)

    barrier = pltpu.get_barrier_semaphore()
    count = 0
    for u, there, _ in others:
        def hello(u=u):
            pl.semaphore_signal(barrier, inc=1, device_id={"tile": u}, device_id_type=MESH)
        when(there, hello)
    for b in range(2):
        for j in range(1, slabs):
            pl.semaphore_signal(
                barrier, inc=1, device_id={"tile": pair + b, "slab": lax.rem(s + j, slabs)}, device_id_type=MESH
            )
    if w == n:
        count = n - 1
    else:
        count = jnp.minimum(t, w - 1) + jnp.minimum(n - 1 - t, w - 1)

    loc_v = pltpu.make_async_copy(v_ref.at[0], vel.at[s, rows(own)], loc_sem.at[0])
    loc_v.start()
    def own_field(ref):
        return pltpu.make_async_copy(ref.at[freq], surf.at[:, rows(own)], loc_sem.at[1])
    pl.when(role == 0)(lambda: own_field(src_ref).start())
    pl.when(role == 1)(lambda: own_field(rcv_ref).start())

    sign = jnp.where(role == 0, -1.0, 1.0).astype(jnp.float32)
    bins = tab_ref.shape[3]
    tabs[...] = jnp.zeros_like(tabs)
    for p in range(2):
        for k in range(terms):
            row = tab_ref[freq, k, pl.ds(p, 1), :]
            if p:
                row = row * sign
            tabs[p * terms + k, :, pl.ds(0, bins)] = jnp.broadcast_to(row, (8, bins))

    pl.semaphore_wait(barrier, count + 2 * (slabs - 1))

    v2 = []

    def spread_slabs(source, slot, x):
        for j in range(1, slabs):
            copy = pltpu.make_async_remote_copy(
                source, vel.at[s, rows(slot)], v2s_sem.at[j, x], v2r_sem.at[s],
                device_id={"slab": lax.rem(s + j, slabs)}, device_id_type=MESH,
            )
            copy.start()
            v2.append(copy)

    def vel_copy(j, u):
        return pltpu.make_async_remote_copy(
            v_ref.at[0], vel.at[s, rows(t - base(u))], v1s_sem.at[j], v1r_sem.at[t - base(u)],
            device_id={"tile": u}, device_id_type=MESH,
        )

    for j, (u, _, needs) in enumerate(others):
        when(needs, lambda j=j, u=u: vel_copy(j, u).start())
    spread_slabs(v_ref.at[0], own, 0)

    def field_copy(ref, j, u):
        return pltpu.make_async_remote_copy(
            ref.at[group + lax.rem(u, 2)], surf.at[:, rows(t - base(u))],
            fs_sem.at[j], fr_sem.at[t - base(u)], device_id={"tile": u}, device_id_type=MESH,
        )

    for j, (u, _, needs) in enumerate(others):
        def send(j=j, u=u):
            pl.when(role == 0)(lambda: field_copy(src_ref, j, u).start())
            pl.when(role == 1)(lambda: field_copy(rcv_ref, j, u).start())
        when(needs, send)

    def flipped(x):
        slot, bit = own, 1
        while bit < w:
            if x & bit:
                slot = slot + bit - 2 * bit * lax.rem(lax.div(own, bit), 2)
            bit *= 2
        return slot

    for x in range(1, w):
        slot = flipped(x)
        pltpu.make_async_remote_copy(
            v_ref.at[0], vel.at[s, rows(slot)], v1s_sem.at[0], v1r_sem.at[slot],
            device_id={"tile": others[0][0]}, device_id_type=MESH,
        ).wait_recv()
        spread_slabs(vel.at[s, rows(slot)], slot, x)
    loc_v.wait()

    own_field(src_ref).wait()
    for j in range(1, w):
        slot = lax.rem(own + j, w)
        pltpu.make_async_remote_copy(
            src_ref.at[0], surf.at[:, rows(slot)], fs_sem.at[0], fr_sem.at[slot],
            device_id={"tile": others[0][0]}, device_id_type=MESH,
        ).wait_recv()

    def window(d):
        reach = (terms - 1) * (slabs - d)
        tops = range(0, wr, 2 * trows) if w == n else [wr]
        size = 0
        for top in tops:
            first, last = (top - reach) // 8 * 8, -(-(top + 2 * trows + reach) // 8) * 8
            if w == n:
                first, last = max(first, 0), min(last, wr)
            size = max(size, last - first)
        size = min(size, wr)
        lowest = (pair - base(t)) * trows - -(-reach // 8) * 8
        return size // 8, pl.multiple_of(jnp.clip(lowest, 0, wr - size), 8)

    def advance(d):
        nbd, start = window(d)
        per = max(g for g in range(1, 9) if nbd % g == 0 and (g <= GROUP or nbd < 8))
        if d == 0:
            for c in range(2):
                for b in range(nb):
                    block = pl.ds(8 * b, 8)
                    even, odd = split_lanes(surf[c, block, pl.ds(0, 128)], surf[c, block, pl.ds(128, 128)])
                    fld[0, c, 0, block, :] = even
                    fld[0, c, 1, block, :] = odd
        terms_of = [
            [
                jnp.concatenate([fld[d, c, h, pl.ds(start + b, 8, stride=nbd), :][None] for b in range(nbd)], axis=0)
                for h in range(2)
            ]
            for c in range(2)
        ]
        changes = [None, None]
        for k in range(terms):
            for c in range(2):
                if k:
                    spread = stencil(terms_of[c])
                    if k == 1:
                        changes[c] = [0.125 * b for b in spread]
                    else:
                        changes[c] = [0.25 * b - e for b, e in zip(spread, changes[c])]
                    terms_of[c] = [e - x for e, x in zip(changes[c], terms_of[c])]
                for h in range(2):
                    tst[k, c, pl.ds(0, nbd), :, pl.ds(128 * h, 128)] = terms_of[c][h]

        @pl.when(s != d)
        def _():
            pltpu.make_async_remote_copy(
                vel.at[d], vel.at[d], v2s_sem.at[0], v2r_sem.at[d],
                device_id={"slab": partner}, device_id_type=MESH,
            ).wait_recv()

        for b in range(nb):
            block = pl.ds(8 * b, 8)
            even, odd = split_lanes(vel[d, block, pl.ds(0, 128)], vel[d, block, pl.ds(128, 128)])
            bins_at[0, block, :] = even
            bins_at[1, block, :] = odd

        def gather(i, _):
            for bb in range(per):
                b = i * per + bb
                block = pl.ds(start + b, 8, stride=nbd)
                for h in range(2):
                    lanes = pl.ds(128 * h, 128)
                    index = bins_at[h, block, :]
                    real = imag = None
                    for k in range(terms):
                        c_real = lane_gather(tabs[k], index)
                        c_imag = lane_gather(tabs[terms + k], index)
                        t_real = tst[k, 0, b, :, lanes]
                        t_imag = tst[k, 1, b, :, lanes]
                        add_real = c_real * t_real - c_imag * t_imag
                        add_imag = c_real * t_imag + c_imag * t_real
                        real = add_real if real is None else real + add_real
                        imag = add_imag if imag is None else imag + add_imag
                    fld[d + 1, 0, h, block, :] = real
                    fld[d + 1, 1, h, block, :] = imag
            return 0

        lax.fori_loop(0, nbd // per, gather, 0)

    mine = rows(pair + role - base(t))
    theirs = rows(pair + (1 - role) - base(t))
    place = lax.div(s, 2) * 2 + low

    def swap(d):
        return pltpu.make_async_remote_copy(
            fld.at[d + 1, :, :, theirs], other.at[d], xs_sem.at[d], xr_sem.at[d],
            device_id={"slab": partner}, device_id_type=MESH,
        )

    def deliver(d):
        return pltpu.make_async_remote_copy(
            part.at[d], contrib.at[place], cs_sem.at[d], cr_sem.at[place],
            device_id={"tile": pair + role, "slab": d}, device_id_type=MESH,
        )

    stays = low == role

    def image(d):
        swap(d).wait_recv()
        product = fld[d + 1, 0, :, mine, :] * other[d, 0] + fld[d + 1, 1, :, mine, :] * other[d, 1]
        home = stays & (s == d)
        @pl.when(home)
        def _():
            contrib[place] = product
        @pl.when(jnp.logical_not(home))
        def _():
            part[d] = product
            deliver(d).start()

    for d in range(slabs):
        advance(d)
        swap(d).start()
        if d:
            image(d - 1)
    image(slabs - 1)

    for q in range(slabs):
        local = (place == q) & stays
        @pl.when(jnp.logical_not(local))
        def _():
            pltpu.make_async_remote_copy(
                part.at[0], contrib.at[q], cs_sem.at[0], cr_sem.at[q],
                device_id={"slab": partner}, device_id_type=MESH,
            ).wait_recv()
    total = contrib[0]
    for q in range(1, slabs):
        total = total + contrib[q]
    for b in range(trows // 8):
        block = pl.ds(8 * b, 8)
        low_half, high_half = merge_lanes(total[0, 8 * b : 8 * b + 8], total[1, 8 * b : 8 * b + 8])
        out_ref[0, block, pl.ds(0, 128)] = low_half
        out_ref[0, block, pl.ds(128, 128)] = high_half

    for copy in v2:
        copy.wait_send()
    for j, (u, _, needs) in enumerate(others):
        def left(j=j, u=u):
            field_copy(src_ref, j, u).wait_send()
            vel_copy(j, u).wait_send()
        when(needs, left)
    for d in range(slabs):
        swap(d).wait_send()
        pl.when(jnp.logical_not(stays & (s == d)))(lambda d=d: deliver(d).wait_send())


def solution(mesh):
    n, slabs = mesh.shape["tile"], mesh.shape["slab"]

    def local(source_field, receiver_field, velocity_index, coefficient_table):
        terms = coefficient_table.shape[2]
        trows, ny = velocity_index.shape[1:]
        reach = -(-(slabs * (terms - 1)) // trows)
        w = min(n, 2 * reach + 2)
        assert source_field.shape[0] == slabs == 4 and n % 2 == 0 and ny == 256
        assert reach == 3 and trows % 8 == 0 and w in (2, 4, 8)
        wr = w * trows
        peers = n - 1 if w == n else 2 * (w - 1)
        dma = pltpu.SemaphoreType.DMA
        anywhere = pl.BlockSpec(memory_space=pl.ANY)
        vmem = pl.BlockSpec(memory_space=pltpu.VMEM)
        return pl.pallas_call(
            functools.partial(kernel, n, slabs, w, trows, terms),
            out_shape=jax.ShapeDtypeStruct((1, trows, ny), jnp.float32),
            in_specs=[anywhere, anywhere, anywhere, vmem],
            out_specs=vmem,
            scratch_shapes=[
                pltpu.VMEM((2, wr, ny), jnp.float32),
                pltpu.VMEM((slabs + 1, 2, 2, wr, ny // 2), jnp.float32),
                pltpu.VMEM((terms, 2, wr // 8, 8, ny), jnp.float32),
                pltpu.VMEM((slabs, wr, ny), jnp.int32),
                pltpu.VMEM((2, wr, ny // 2), jnp.int32),
                pltpu.VMEM((2 * terms, 8, 128), jnp.float32),
                pltpu.VMEM((slabs, 2, 2, trows, ny // 2), jnp.float32),
                pltpu.VMEM((slabs, 2, trows, ny // 2), jnp.float32),
                pltpu.VMEM((slabs, 2, trows, ny // 2), jnp.float32),
                dma((2,)),
                dma((peers,)),
                dma((w,)),
                dma((peers,)),
                dma((w,)),
                dma((slabs, w)),
                dma((slabs,)),
                dma((slabs,)),
                dma((slabs,)),
                dma((slabs,)),
                dma((slabs,)),
            ],
            compiler_params=pltpu.CompilerParams(collective_id=0, has_side_effects=True),
            name="migrate",
        )(source_field, receiver_field, velocity_index, jnp.transpose(coefficient_table, (0, 2, 1, 3)))

    return jax.shard_map(
        local,
        mesh=mesh,
        in_specs=(
            P("shot", None, "tile", None),
            P("shot", None, "tile", None),
            P(("shot", "slab"), "tile", None),
            P(),
        ),
        out_specs=P(("shot", "slab"), "tile", None),
        check_vma=False,
    )
```
